32 devices in a mesh: clip: 2 (over x), ord: 16 (over z, y, core).
Axes of the slice: x: 2, y: 2, z: 4, core: 2. Of those that a mesh axis runs over, the one named last changes fastest.
Arguments:
- reflection: bfloat16 [2, 16384, 8192], P(None, ('clip', 'ord')), parts along dimension 1, may hold values from -0.0625 to 0.0625
- incidence: bfloat16 [2, 8192, 16], replicated, may hold values from -6 to 6
- source_shift: int32 [16, 2], P('ord'), may hold values from -8 to 8
- source_weight: float32 [16], P('ord'), may hold values from 0.1 to 1
- grid_map: int32 [4096], replicated, may hold values from 0 to 4095, each once
- pupil_mask: int32 [64, 64], replicated, may hold values 0 or 1
- pupil_phase: float32 [2, 64, 64], replicated, may hold values from -3.140625 to 3.140625
- tile_order: int32 [16], replicated, may hold values from 0 to 15, each once
Outputs:
- aerial: float32 [2048, 2, 1024], P(('clip', 'ord')), parts along dimension 0
The draws below stay inside these ranges and needn't reach their ends.
There are 2 independent parts, one for each index of `clip`. The reference program is written for one: setup_inputs(seed, part) draws one part's arguments, and reference() takes and returns one part's arrays. A program takes and returns all parts, laid end to end along the dimension named above; an argument that names none is the same for every part. Nothing has to cross between parts.
Inputs may be any that keep to these rules, and one draw needn't show every extreme that they name: `grid_map`: a permutation of the 4096 pupil cells. `tile_order`: a permutation of the 16 tiles.
All inputs are finite; a program needn't handle non-finite values.
Results may differ from the reference program's by a relative error of at most 0.0003.
Values may be sent and summed in bfloat16 or wider, within the bound.
A program may use at most 128 MiB of HBM per device.

```python
import math
import jax
import jax.numpy as jnp
from jax import lax

G = 64
NORD = 4096
ORD2 = 8192
PIX = 1024
SOURCES = 16
TILES = 16
SHIFT = 8


def place_ends(values, own_key, smallest, high):
    extent = values.shape
    index_at = [jax.random.randint(jax.random.fold_in(own_key, axis), (), 0, extent[axis]) for axis in range(len(extent))]
    values = values.at[tuple(index_at)].set(smallest)
    longest = extent.index(max(extent))
    index_at[longest] = (index_at[longest] + 1) % extent[longest]
    return values.at[tuple(index_at)].set(high)


def steps_of(stream_key, dims, split, low, largest):
    gain = 1.0
    for axis_at, shards_of in split:
        draws = jax.random.uniform(jax.random.fold_in(jax.random.fold_in(stream_key, 6), axis_at), (shards_of,), jnp.float32, low / len(split), largest / len(split))
        gain = gain * jnp.repeat(jnp.exp(draws), dims[axis_at] // shards_of).reshape((-1,) + (1,) * (len(dims) - 1 - axis_at))
    return gain


def noise(own_key, dims, spread, most, split=(), kind=jnp.bfloat16):
    values = jax.random.normal(own_key, dims, jnp.float32) * spread
    if len(split) > 0:
        values = steps_of(own_key, dims, split, -0.22, 0.18) * values
    return jnp.clip(values, min=-most, max=most).astype(kind)


def setup_inputs(seed: int = 0, part: int = 0) -> dict:
    key_of = jax.random.split(jax.random.key(seed), 9)
    part_splits = jax.random.split(jax.random.fold_in(key_of[8], part), 9)
    return {
        "reflection": noise(part_splits[0], (2, ORD2, ORD2), ORD2 ** -0.5, 0.0625, ((1, 16),)),
        "incidence": noise(key_of[1], (2, ORD2, SOURCES), 1.0, 6.0),
        "source_shift": place_ends(jax.random.randint(key_of[2], (SOURCES, 2), -SHIFT, SHIFT + 1), jax.random.fold_in(key_of[2], 1), -SHIFT, SHIFT).astype(jnp.int32),
        "source_weight": jnp.clip(jnp.exp(math.log(1.0) - 2.3025851 * jax.random.uniform(key_of[3], (SOURCES,), jnp.float32) ** steps_of(key_of[3], (SOURCES,), ((0, 16),), -0.2, 0.2)), 0.1, 1.0),
        "grid_map": jax.random.permutation(key_of[4], NORD).astype(jnp.int32),
        "pupil_mask": place_ends((jax.random.randint(key_of[5], (G, G), 0, 4) < 3).astype(jnp.int32), jax.random.fold_in(key_of[5], 1), 0, 1),
        "pupil_phase": jnp.clip(jax.random.uniform(key_of[6], (2, G, G), jnp.float32, -3.140625, 3.140625), -3.140625, 3.140625),
        "tile_order": jax.random.permutation(key_of[7], TILES).astype(jnp.int32),
    }


HIGHEST = lax.Precision.HIGHEST

def phase_table(left_ints, right_ints, period):
    turn_index = jnp.mod(left_ints[:, None] * right_ints[None, :], period).astype(jnp.float32)
    angles = turn_index * (2.0 * math.pi / period)
    return (jnp.cos(angles), jnp.sin(angles))

def band_kernel(points, period, grid_side):
    samples = 2 * grid_side
    difference = jnp.arange(1 - grid_side, grid_side, dtype=jnp.int32)
    fine_cos, fine_sin = phase_table(points, difference, period)
    coarse_cos, coarse_sin = phase_table(jnp.arange(samples, dtype=jnp.int32), difference, samples)
    joined = jnp.einsum('pm,cm->pc', fine_cos, coarse_cos, precision=HIGHEST)
    joined = joined + jnp.einsum('pm,cm->pc', fine_sin, coarse_sin, precision=HIGHEST)
    return joined / samples

def reference(reflection, incidence, source_shift, source_weight, grid_map, pupil_mask, pupil_phase, tile_order):
    grid_side = pupil_mask.shape[0]
    order_count = grid_side * grid_side
    source_count = incidence.shape[2]
    real_part = (jnp.dot(reflection[0], incidence[0], preferred_element_type=jnp.float32) - jnp.dot(reflection[1], incidence[1], preferred_element_type=jnp.float32)).astype(jnp.bfloat16)
    imag_part = (jnp.dot(reflection[0], incidence[1], preferred_element_type=jnp.float32) + jnp.dot(reflection[1], incidence[0], preferred_element_type=jnp.float32)).astype(jnp.bfloat16)
    inverse = jnp.argsort(grid_map).astype(jnp.int32)

    def to_cells(values):
        ordered = jnp.take(values.astype(jnp.float32).reshape(2, order_count, source_count), inverse, axis=1)
        return jnp.transpose(ordered.reshape(2, grid_side, grid_side, source_count), (3, 0, 1, 2))
    cell_real = to_cells(real_part)
    cell_imag = to_cells(imag_part)
    margin = grid_side // 8
    open_pad = jnp.pad(pupil_mask.astype(jnp.float32), margin)
    phase_pad = jnp.pad(pupil_phase, ((0, 0), (margin, margin), (margin, margin)))

    def window(one_shift):
        row_start = (margin + one_shift[0]).astype(jnp.int32)
        col_start = (margin + one_shift[1]).astype(jnp.int32)
        opened = lax.dynamic_slice(open_pad, (row_start, col_start), (grid_side, grid_side))
        phased = lax.dynamic_slice(phase_pad, (jnp.zeros((), jnp.int32), row_start, col_start), (2, grid_side, grid_side))
        return (opened, phased)
    opened, phased = jax.vmap(window)(source_shift)
    phase_cos = jnp.cos(phased)[:, :, None]
    phase_sin = jnp.sin(phased)[:, :, None]
    open_scale = opened[:, None, None] * (1.0 / math.sqrt(order_count))
    amp_real = (cell_real[:, None] * phase_cos - cell_imag[:, None] * phase_sin) * open_scale
    amp_imag = (cell_real[:, None] * phase_sin + cell_imag[:, None] * phase_cos) * open_scale
    samples = 2 * grid_side
    frequency = jnp.arange(grid_side, dtype=jnp.int32) - grid_side // 2
    cosine, sine = phase_table(jnp.arange(samples, dtype=jnp.int32), frequency, samples)
    half_real = jnp.einsum('sfpyg,cg->sfpyc', amp_real, cosine, precision=HIGHEST) - jnp.einsum('sfpyg,cg->sfpyc', amp_imag, sine, precision=HIGHEST)
    half_imag = jnp.einsum('sfpyg,cg->sfpyc', amp_real, sine, precision=HIGHEST) + jnp.einsum('sfpyg,cg->sfpyc', amp_imag, cosine, precision=HIGHEST)
    full_real = jnp.einsum('ry,sfpyc->sfprc', cosine, half_real, precision=HIGHEST) - jnp.einsum('ry,sfpyc->sfprc', sine, half_imag, precision=HIGHEST)
    full_imag = jnp.einsum('ry,sfpyc->sfprc', sine, half_real, precision=HIGHEST) + jnp.einsum('ry,sfpyc->sfprc', cosine, half_imag, precision=HIGHEST)
    powers = jnp.einsum('s,sfprc->rfc', source_weight / source_count, full_real * full_real + full_imag * full_imag, precision=HIGHEST)
    tile_rows = PIX // tile_order.shape[0]
    all_rows = jnp.arange(PIX, dtype=jnp.int32)
    image_rows = tile_order[all_rows // tile_rows] * tile_rows + all_rows % tile_rows
    kernel_rows = band_kernel(image_rows, PIX, grid_side)
    kernel_cols = band_kernel(all_rows, PIX, grid_side)
    partial_value = jnp.einsum('rc,cfd->rfd', kernel_rows, powers, precision=HIGHEST)
    return jnp.einsum('rfd,xd->rfx', partial_value, kernel_cols, precision=HIGHEST)
```

```python
import functools
import math

import jax
import jax.numpy as jnp
import numpy as np
from jax import lax
from jax.experimental import pallas as pl
from jax.experimental.pallas import tpu as pltpu
from jax.sharding import PartitionSpec as P

PIX = 1024
HIGHEST = lax.Precision.HIGHEST
NN = (((1,), (0,)), ((), ()))
NT = (((1,), (1,)), ((), ()))
MESH = pl.DeviceIdType.MESH


def turn_table(left, right, period):
    angles = np.mod(np.outer(left, right), period) * (2.0 * math.pi / period)
    return np.cos(angles), np.sin(angles)


def split_const(values):
    values = np.asarray(values, np.float32)
    high = values.astype(jnp.bfloat16)
    low = (values - high.astype(np.float32)).astype(jnp.bfloat16)
    return np.stack([high, low])


def lift_tables(grid_side):
    samples = 2 * grid_side
    frequency = np.arange(grid_side) - grid_side // 2
    cosine, sine = turn_table(frequency, np.arange(samples), samples)
    cols = np.block([[cosine, sine], [-sine, cosine]])
    rows = np.block([[cosine.T, -sine.T], [sine.T, cosine.T]])
    return split_const(cols), split_const(rows)


def band_table(pixels, grid_side):
    samples = 2 * grid_side
    difference = np.arange(1 - grid_side, grid_side)
    fine_cos, fine_sin = turn_table(np.arange(pixels), difference, pixels)
    coarse_cos, coarse_sin = turn_table(np.arange(samples), difference, samples)
    return split_const((fine_cos @ coarse_cos.T + fine_sin @ coarse_sin.T) / samples)


def split(values):
    high = values.astype(jnp.bfloat16)
    low = (values - high.astype(jnp.float32)).astype(jnp.bfloat16)
    return high, low


def dot3(left, right, dims):
    dot = functools.partial(lax.dot_general, dimension_numbers=dims, preferred_element_type=jnp.float32)
    return dot(left[0], right[0]) + (dot(left[0], right[1]) + dot(left[1], right[0]))


def optics_kernel(
    shift_ref,
    weight_ref,
    reflection_ref,
    incidence_ref,
    cells_ref,
    mask_ref,
    phase_ref,
    cols_ref,
    rows_ref,
    out_ref,
    refl_buf,
    inc_buf,
    acc_ref,
    send_buf,
    recv_buf,
    grid_acc,
    part_buf,
    gather_buf,
    load_sem,
    own_sem,
    a_send,
    a_recv,
    r_send,
    r_recv,
    g_send,
    g_recv,
    *,
    devices,
    chunks,
):
    me = lax.axis_index("ord")
    sources = inc_buf.shape[2]
    side = mask_ref.shape[0]
    samples = 2 * side
    depth = refl_buf.shape[2] // chunks

    def loads(c):
        span = pl.ds(c * depth, depth)
        return (
            pltpu.make_async_copy(incidence_ref.at[:, span, :], inc_buf.at[:, span, :], load_sem.at[0, c]),
            pltpu.make_async_copy(reflection_ref.at[:, :, span], refl_buf.at[:, :, span], load_sem.at[1, c]),
        )

    for c in range(chunks):
        for load in loads(c):
            load.start()

    barrier = pltpu.get_barrier_semaphore()

    def greet(j, carry):
        pl.semaphore_signal(barrier, inc=1, device_id={"ord": lax.rem(me + j, devices)}, device_id_type=MESH)
        return carry

    lax.fori_loop(1, devices, greet, 0)

    shift_y = shift_ref[0, 0]
    shift_x = shift_ref[0, 1]
    opened = mask_ref[...].astype(jnp.float32) * (1.0 / side)
    planes = []
    for f in range(2):
        planes += [jnp.cos(phase_ref[f]) * opened, jnp.sin(phase_ref[f]) * opened]
    row_at = lax.broadcasted_iota(jnp.int32, (side, side), 0)
    col_at = lax.broadcasted_iota(jnp.int32, (side, side), 1)
    pick_row = jnp.where(col_at == row_at + shift_y, 1.0, 0.0)
    from_at = lax.broadcasted_iota(jnp.int32, (side, 2 * side), 0)
    to_at = lax.broadcasted_iota(jnp.int32, (side, 2 * side), 1)
    half = jnp.where(to_at >= side, 1, 0)
    hit = from_at == to_at - half * side + shift_x
    pick_cos = jnp.where(hit, 1.0, 0.0)
    pick_sin = jnp.where(hit, jnp.where(half == 1, 1.0, -1.0), 0.0)
    windows = []
    for f in range(2):
        for kind, pick in ((0, pick_cos), (1, pick_sin)):
            moved = lax.dot_general(pick_row, planes[2 * f + kind], NN, precision=HIGHEST, preferred_element_type=jnp.float32)
            windows.append(lax.dot_general(moved, pick, NN, precision=HIGHEST, preferred_element_type=jnp.float32))

    for c in range(chunks):
        inc_load, refl_load = loads(c)
        span = pl.ds(c * depth, depth)
        inc_load.wait()
        first = inc_buf[0, span, :]
        second = inc_buf[1, span, :]
        join_a = jnp.concatenate([first, second], 1)
        join_b = jnp.concatenate([-second, first], 1)
        refl_load.wait()
        step = jnp.dot(refl_buf[0, :, span], join_a, preferred_element_type=jnp.float32)
        step = step + jnp.dot(refl_buf[1, :, span], join_b, preferred_element_type=jnp.float32)
        if c == 0:
            acc_ref[...] = step
        else:
            acc_ref[...] += step

    lanes = 2 * sources
    to_row = lax.broadcasted_iota(jnp.int32, (lanes, lanes), 0)
    from_col = lax.broadcasted_iota(jnp.int32, (lanes, lanes), 1)
    turned = jnp.where(from_col == to_row // 2 + (to_row % 2) * sources, 1.0, 0.0).astype(jnp.bfloat16)
    by_source = lax.dot_general(
        turned, acc_ref[...].astype(jnp.bfloat16), NT, preferred_element_type=jnp.float32
    )
    for s in range(sources):
        send_buf[s] = by_source[2 * s : 2 * s + 2].astype(jnp.bfloat16)

    pl.semaphore_wait(barrier, devices - 1)

    def fan(source_of, target, send_sem, recv_sem):
        def copy_to(peer, sender):
            return pltpu.make_async_remote_copy(
                src_ref=source_of(peer),
                dst_ref=target.at[sender],
                send_sem=send_sem.at[peer],
                recv_sem=recv_sem.at[sender],
                device_id={"ord": peer},
                device_id_type=MESH,
            )

        def start(j, carry):
            copy_to(lax.rem(me + j, devices), me).start()
            return carry

        def wait_recv(sender):
            copy_to(sender, sender).wait_recv()

        def drain(j, carry):
            copy_to(lax.rem(me + j, devices), me).wait_send()
            return carry

        return start, wait_recv, drain

    start, wait_recv, drain_a = fan(lambda d: send_buf.at[d], recv_buf, a_send, a_recv)
    own = pltpu.make_async_copy(send_buf.at[me], recv_buf.at[me], own_sem.at[0])
    own.start()
    lax.fori_loop(1, devices, start, 0)

    grid_acc[...] = jnp.zeros_like(grid_acc)
    local_rows = recv_buf.shape[2]
    per_pol = devices // 2
    cell_at = lax.broadcasted_iota(jnp.int32, (side, local_rows), 0)

    own.wait()

    def take(j, carry):
        r = lax.rem(me + j, devices)

        @pl.when(j > 0)
        def _():
            wait_recv(r)

        p = r // per_pol
        cells = cells_ref[lax.rem(r, per_pol)]
        cell_y = cells // side
        hit_y = jnp.where(cell_at == cell_y, 1.0, 0.0).astype(jnp.bfloat16)
        hit_x = cell_at == cells - cell_y * side
        values = recv_buf[r].astype(jnp.float32)
        spread = jnp.concatenate(
            [jnp.where(hit_x, values[0:1], 0.0), jnp.where(hit_x, values[1:2], 0.0)], 0
        ).astype(jnp.bfloat16)
        grid_acc[p] += lax.dot_general(hit_y, spread, NT, preferred_element_type=jnp.float32)
        return carry

    lax.fori_loop(0, devices, take, 0)

    amps = []
    for f in range(2):
        for p in range(2):
            cells = grid_acc[p]
            swapped = jnp.concatenate([cells[:, side:], cells[:, :side]], 1)
            amps.append(cells * windows[2 * f] + swapped * windows[2 * f + 1])
    stacked = split(jnp.concatenate(amps, 0))
    halves = dot3(stacked, (cols_ref[0], cols_ref[1]), NN)
    columns = jnp.concatenate(
        [
            jnp.concatenate(
                [
                    halves[i * side : (i + 1) * side, :samples],
                    halves[i * side : (i + 1) * side, samples:],
                ],
                0,
            )
            for i in range(4)
        ],
        1,
    )
    fields = dot3((rows_ref[0], rows_ref[1]), split(columns), NN)
    powers = fields[:samples] * fields[:samples] + fields[samples:] * fields[samples:]
    weight = weight_ref[0] * (1.0 / sources)
    summed = (
        jnp.concatenate(
            [
                powers[:, :samples] + powers[:, samples : 2 * samples],
                powers[:, 2 * samples : 3 * samples] + powers[:, 3 * samples :],
            ],
            1,
        )
        * weight
    )
    part_rows = part_buf.shape[1]
    part_buf[...] = summed.reshape(devices, part_rows, 2 * samples)

    start, wait_recv_r, drain_r = fan(lambda d: part_buf.at[d], gather_buf.at[0], r_send, r_recv)
    lax.fori_loop(1, devices, start, 0)

    def add(j, total):
        r = lax.rem(me + j, devices)
        wait_recv_r(r)
        return total + gather_buf[0, r]

    total = lax.fori_loop(1, devices, add, part_buf[me])
    gather_buf[1, me] = total

    start, wait_recv_g, drain_g = fan(lambda d: gather_buf.at[1, me], gather_buf.at[1], g_send, g_recv)
    lax.fori_loop(1, devices, start, 0)

    def arrive(j, carry):
        wait_recv_g(lax.rem(me + j, devices))
        return carry

    lax.fori_loop(1, devices, arrive, 0)
    out_ref[...] = gather_buf[1].reshape(samples, 2 * samples)
    lax.fori_loop(1, devices, drain_a, 0)
    lax.fori_loop(1, devices, drain_r, 0)
    lax.fori_loop(1, devices, drain_g, 0)


def image_kernel(tile_ref, rows_ref, cols_ref, samples_ref, out_ref):
    samples = cols_ref.shape[2]
    partial = dot3((rows_ref[0], rows_ref[1]), split(samples_ref[...]), NN)
    for f in range(2):
        piece = split(partial[:, f * samples : (f + 1) * samples])
        out_ref[:, f, :] = dot3(piece, (cols_ref[0], cols_ref[1]), NT)


def local(
    reflection,
    incidence,
    source_shift,
    source_weight,
    grid_map,
    pupil_mask,
    pupil_phase,
    tile_order,
):
    devices = lax.axis_size("ord")
    local_rows = reflection.shape[1]
    order2 = reflection.shape[2]
    sources = incidence.shape[2]
    side = pupil_mask.shape[0]
    samples = 2 * side
    assert source_shift.shape[0] == 1 and sources == devices
    chunks = 8
    cols, rows = lift_tables(side)
    table = band_table(PIX, side)
    vmem = pl.BlockSpec(memory_space=pltpu.VMEM)
    smem = pl.BlockSpec(memory_space=pltpu.SMEM)
    anywhere = pl.BlockSpec(memory_space=pl.ANY)
    part_rows = samples // devices
    dma = pltpu.SemaphoreType.DMA
    summed = pl.pallas_call(
        functools.partial(optics_kernel, devices=devices, chunks=chunks),
        out_shape=jax.ShapeDtypeStruct((samples, 2 * samples), jnp.float32),
        in_specs=[smem, smem, anywhere, anywhere, vmem, vmem, vmem, vmem, vmem],
        out_specs=vmem,
        scratch_shapes=[
            pltpu.VMEM((2, local_rows, order2), jnp.bfloat16),
            pltpu.VMEM((2, order2, sources), jnp.bfloat16),
            pltpu.VMEM((local_rows, 2 * sources), jnp.float32),
            pltpu.VMEM((devices, 2, local_rows), jnp.bfloat16),
            pltpu.VMEM((devices, 2, local_rows), jnp.bfloat16),
            pltpu.VMEM((2, side, samples), jnp.float32),
            pltpu.VMEM((devices, part_rows, 2 * samples), jnp.float32),
            pltpu.VMEM((2, devices, part_rows, 2 * samples), jnp.float32),
            dma((2, chunks)),
            dma((1,)),
            dma((devices,)),
            dma((devices,)),
            dma((devices,)),
            dma((devices,)),
            dma((devices,)),
            dma((devices,)),
        ],
        compiler_params=pltpu.CompilerParams(
            collective_id=0, has_side_effects=True, vmem_limit_bytes=48 * 1024 * 1024
        ),
    )(
        source_shift,
        source_weight,
        reflection,
        incidence,
        grid_map.reshape(devices // 2, 1, local_rows),
        pupil_mask,
        pupil_phase,
        jnp.asarray(cols),
        jnp.asarray(rows),
    )
    tile_rows = PIX // devices
    tile = lax.dynamic_slice(tile_order, (lax.axis_index("ord"),), (1,))
    return pl.pallas_call(
        image_kernel,
        out_shape=jax.ShapeDtypeStruct((tile_rows, 2, PIX), jnp.float32),
        grid_spec=pltpu.PrefetchScalarGridSpec(
            num_scalar_prefetch=1,
            grid=(1,),
            in_specs=[
                pl.BlockSpec((2, tile_rows, samples), lambda i, t: (0, t[0], 0)),
                pl.BlockSpec((2, PIX, samples), lambda i, t: (0, 0, 0)),
                pl.BlockSpec((samples, 2 * samples), lambda i, t: (0, 0)),
            ],
            out_specs=pl.BlockSpec((tile_rows, 2, PIX), lambda i, t: (0, 0, 0)),
        ),
    )(tile, jnp.asarray(table), jnp.asarray(table), summed)


def solution(mesh):
    in_specs = (P(None, ("clip", "ord"), None), P(), P("ord", None), P("ord"), P(), P(), P(), P())
    out_specs = P(("clip", "ord"), None, None)
    return jax.shard_map(local, mesh=mesh, in_specs=in_specs, out_specs=out_specs, check_vma=False)
```

```python
import functools
import math

import jax
import jax.numpy as jnp
import numpy as np
from jax import lax
from jax.experimental import pallas as pl
from jax.experimental.pallas import tpu as pltpu
from jax.sharding import PartitionSpec as P

PIX = 1024
HIGHEST = lax.Precision.HIGHEST
NN = (((1,), (0,)), ((), ()))
NT = (((1,), (1,)), ((), ()))
MESH = pl.DeviceIdType.MESH


def turn_table(left, right, period):
    angles = np.mod(np.outer(left, right), period) * (2.0 * math.pi / period)
    return np.cos(angles), np.sin(angles)


def split_const(values):
    values = np.asarray(values, np.float32)
    high = values.astype(jnp.bfloat16)
    low = (values - high.astype(np.float32)).astype(jnp.bfloat16)
    return np.stack([high, low])


def lift_tables(grid_side):
    samples = 2 * grid_side
    frequency = np.arange(grid_side) - grid_side // 2
    cosine, sine = turn_table(frequency, np.arange(samples), samples)
    cols = np.block([[cosine, sine], [-sine, cosine]])
    rows = np.block([[cosine.T, -sine.T], [sine.T, cosine.T]])
    return split_const(cols), split_const(rows)


def band_table(pixels, grid_side):
    samples = 2 * grid_side
    difference = np.arange(1 - grid_side, grid_side)
    fine_cos, fine_sin = turn_table(np.arange(pixels), difference, pixels)
    coarse_cos, coarse_sin = turn_table(np.arange(samples), difference, samples)
    return np.concatenate(split_const((fine_cos @ coarse_cos.T + fine_sin @ coarse_sin.T) / samples), 1)


def split(values):
    high = values.astype(jnp.bfloat16)
    low = (values - high.astype(jnp.float32)).astype(jnp.bfloat16)
    return high, low


def dot3(left, right, dims):
    dot = functools.partial(lax.dot_general, dimension_numbers=dims, preferred_element_type=jnp.float32)
    return dot(left[0], right[0]) + (dot(left[0], right[1]) + dot(left[1], right[0]))


def optics_kernel(
    shift_hbm,
    weight_hbm,
    reflection_ref,
    incidence_ref,
    cells_hbm,
    mask_hbm,
    phase_hbm,
    cols_hbm,
    rows_hbm,
    tile_hbm,
    band_rows_hbm,
    band_cols_hbm,
    out_hbm,
    shift_ref,
    weight_ref,
    cells_ref,
    mask_ref,
    phase_ref,
    cols_ref,
    rows_ref,
    tile_ref,
    band_rows_ref,
    band_cols_ref,
    image_ref,
    refl_buf,
    inc_buf,
    acc_ref,
    send_buf,
    recv_buf,
    grid_acc,
    part_buf,
    gather_buf,
    load_sem,
    small_sem,
    own_sem,
    a_send,
    a_recv,
    r_send,
    r_recv,
    g_send,
    g_recv,
    out_sem,
    *,
    devices,
    chunks,
):
    me = lax.axis_index("ord")
    sources = inc_buf.shape[1]
    side = mask_ref.shape[0]
    samples = 2 * side
    depth = refl_buf.shape[2] // chunks

    def loads(c):
        span = pl.ds(c * depth, depth)
        return (
            pltpu.make_async_copy(incidence_ref.at[:, :, span], inc_buf.at[:, :, span], load_sem.at[0, c]),
            pltpu.make_async_copy(reflection_ref.at[:, :, span], refl_buf.at[:, :, span], load_sem.at[1, c]),
        )

    smalls = [
        pltpu.make_async_copy(source, target, small_sem.at[i])
        for i, (source, target) in enumerate(
            (
                (shift_hbm, shift_ref),
                (mask_hbm, mask_ref),
                (phase_hbm, phase_ref),
                (weight_hbm, weight_ref),
                (cells_hbm, cells_ref),
                (cols_hbm, cols_ref),
                (rows_hbm, rows_ref),
                (tile_hbm, tile_ref),
                (band_rows_hbm, band_rows_ref),
                (band_cols_hbm, band_cols_ref),
            )
        )
    ]
    for small in smalls[:3]:
        small.start()
    for c in range(chunks):
        for load in loads(c):
            load.start()
    for small in smalls[3:]:
        small.start()

    barrier = pltpu.get_barrier_semaphore()

    def greet(j, carry):
        pl.semaphore_signal(barrier, inc=1, device_id={"ord": lax.rem(me + j, devices)}, device_id_type=MESH)
        return carry

    lax.fori_loop(1, devices, greet, 0)

    for small in smalls[:3]:
        small.wait()
    shift_y = shift_ref[0, 0]
    shift_x = shift_ref[0, 1]
    opened = mask_ref[...].astype(jnp.float32) * (1.0 / side)
    planes = []
    for f in range(2):
        planes += [jnp.cos(phase_ref[f]) * opened, jnp.sin(phase_ref[f]) * opened]
    row_at = lax.broadcasted_iota(jnp.int32, (side, side), 0)
    col_at = lax.broadcasted_iota(jnp.int32, (side, side), 1)
    pick_row = jnp.where(col_at == row_at + shift_y, 1.0, 0.0)
    from_at = lax.broadcasted_iota(jnp.int32, (side, 2 * side), 0)
    to_at = lax.broadcasted_iota(jnp.int32, (side, 2 * side), 1)
    half = jnp.where(to_at >= side, 1, 0)
    hit = from_at == to_at - half * side + shift_x
    pick_cos = jnp.where(hit, 1.0, 0.0)
    pick_sin = jnp.where(hit, jnp.where(half == 1, 1.0, -1.0), 0.0)
    windows = []
    for f in range(2):
        for kind, pick in ((0, pick_cos), (1, pick_sin)):
            moved = lax.dot_general(pick_row, planes[2 * f + kind], NN, precision=HIGHEST, preferred_element_type=jnp.float32)
            windows.append(lax.dot_general(moved, pick, NN, precision=HIGHEST, preferred_element_type=jnp.float32))

    for c in range(chunks):
        inc_load, refl_load = loads(c)
        span = pl.ds(c * depth, depth)
        inc_load.wait()
        first = inc_buf[0, :, span]
        second = inc_buf[1, :, span]
        join_a = jnp.concatenate([first, second], 0)
        join_b = jnp.concatenate([-second, first], 0)
        refl_load.wait()
        step = lax.dot_general(refl_buf[0, :, span], join_a, NT, preferred_element_type=jnp.float32)
        step = step + lax.dot_general(refl_buf[1, :, span], join_b, NT, preferred_element_type=jnp.float32)
        if c == 0:
            acc_ref[...] = step
        else:
            acc_ref[...] += step

    lanes = 2 * sources
    to_row = lax.broadcasted_iota(jnp.int32, (lanes, lanes), 0)
    from_col = lax.broadcasted_iota(jnp.int32, (lanes, lanes), 1)
    turned = jnp.where(from_col == to_row // 2 + (to_row % 2) * sources, 1.0, 0.0).astype(jnp.bfloat16)
    by_source = lax.dot_general(
        turned, acc_ref[...].astype(jnp.bfloat16), NT, preferred_element_type=jnp.float32
    )
    for s in range(sources):
        send_buf[s] = by_source[2 * s : 2 * s + 2].astype(jnp.bfloat16)

    pl.semaphore_wait(barrier, devices - 1)

    def fan(source_of, target, send_sem, recv_sem):
        def copy_to(peer, sender):
            return pltpu.make_async_remote_copy(
                src_ref=source_of(peer),
                dst_ref=target.at[sender],
                send_sem=send_sem.at[peer],
                recv_sem=recv_sem.at[sender],
                device_id={"ord": peer},
                device_id_type=MESH,
            )

        def start(j, carry):
            copy_to(lax.rem(me + j, devices), me).start()
            return carry

        def wait_recv(sender):
            copy_to(sender, sender).wait_recv()

        def drain(j, carry):
            copy_to(lax.rem(me + j, devices), me).wait_send()
            return carry

        return start, wait_recv, drain

    start, wait_recv, drain_a = fan(lambda d: send_buf.at[d], recv_buf, a_send, a_recv)
    for small in smalls[3:]:
        small.wait()
    own = pltpu.make_async_copy(send_buf.at[me], recv_buf.at[me], own_sem.at[0])
    own.start()
    lax.fori_loop(1, devices, start, 0)

    grid_acc[...] = jnp.zeros_like(grid_acc)
    local_rows = recv_buf.shape[2]
    per_pol = devices // 2
    cell_at = lax.broadcasted_iota(jnp.int32, (side, local_rows), 0)

    own.wait()

    def take(j, carry):
        r = lax.rem(me + j, devices)

        @pl.when(j > 0)
        def _():
            wait_recv(r)

        p = r // per_pol
        cells = cells_ref[lax.rem(r, per_pol)]
        cell_y = cells // side
        hit_y = jnp.where(cell_at == cell_y, 1.0, 0.0).astype(jnp.bfloat16)
        hit_x = cell_at == cells - cell_y * side
        values = recv_buf[r].astype(jnp.float32)
        spread = jnp.concatenate(
            [jnp.where(hit_x, values[0:1], 0.0), jnp.where(hit_x, values[1:2], 0.0)], 0
        ).astype(jnp.bfloat16)
        grid_acc[p] += lax.dot_general(hit_y, spread, NT, preferred_element_type=jnp.float32)
        return carry

    lax.fori_loop(0, devices, take, 0)

    amps = []
    for f in range(2):
        for p in range(2):
            cells = grid_acc[p]
            swapped = jnp.concatenate([cells[:, side:], cells[:, :side]], 1)
            amps.append(cells * windows[2 * f] + swapped * windows[2 * f + 1])
    stacked = split(jnp.concatenate(amps, 0))
    halves = dot3(stacked, (cols_ref[0], cols_ref[1]), NN)
    columns = jnp.concatenate(
        [
            jnp.concatenate(
                [
                    halves[i * side : (i + 1) * side, :samples],
                    halves[i * side : (i + 1) * side, samples:],
                ],
                0,
            )
            for i in range(4)
        ],
        1,
    )
    fields = dot3((rows_ref[0], rows_ref[1]), split(columns), NN)
    powers = fields[:samples] * fields[:samples] + fields[samples:] * fields[samples:]
    weight = weight_ref[0, 0] * (1.0 / sources)
    summed = (
        jnp.concatenate(
            [
                powers[:, :samples] + powers[:, samples : 2 * samples],
                powers[:, 2 * samples : 3 * samples] + powers[:, 3 * samples :],
            ],
            1,
        )
        * weight
    )
    part_rows = part_buf.shape[1]
    part_buf[...] = summed.reshape(devices, part_rows, 2 * samples)

    start, wait_recv_r, drain_r = fan(lambda d: part_buf.at[d], gather_buf.at[0], r_send, r_recv)
    lax.fori_loop(1, devices, start, 0)

    def add(j, total):
        r = lax.rem(me + j, devices)
        wait_recv_r(r)
        return total + gather_buf[0, r]

    total = lax.fori_loop(1, devices, add, part_buf[me])
    gather_buf[1, me] = total

    start, wait_recv_g, drain_g = fan(lambda d: gather_buf.at[1, me], gather_buf.at[1], g_send, g_recv)
    lax.fori_loop(1, devices, start, 0)

    def arrive(j, carry):
        wait_recv_g(lax.rem(me + j, devices))
        return carry

    lax.fori_loop(1, devices, arrive, 0)
    tile_rows, _, pixels = image_ref.shape
    pieces = out_sem.shape[0]
    lift = band_rows_ref[tile_ref[me]]
    high, low = split(gather_buf[1].reshape(samples, 2 * samples))
    partial = jnp.dot(lift, jnp.concatenate([high, high], 0), preferred_element_type=jnp.float32)
    partial = partial + jnp.dot(lift[:, :samples], low, preferred_element_type=jnp.float32)
    high, low = split(jnp.concatenate([partial[:, :samples], partial[:, samples:]], 0))
    twice = jnp.concatenate([high, high], 1)
    width = pixels // pieces
    stores = []
    for i in range(pieces):
        span = pl.ds(i * width, width)
        table = band_cols_ref[span, :]
        piece = lax.dot_general(twice, table, NT, preferred_element_type=jnp.float32)
        piece = piece + lax.dot_general(low, table[:, :samples], NT, preferred_element_type=jnp.float32)
        image_ref[:, 0, span] = piece[:tile_rows]
        image_ref[:, 1, span] = piece[tile_rows:]
        store = pltpu.make_async_copy(image_ref.at[:, :, span], out_hbm.at[:, :, span], out_sem.at[i])
        store.start()
        stores.append(store)
    lax.fori_loop(1, devices, drain_a, 0)
    lax.fori_loop(1, devices, drain_r, 0)
    lax.fori_loop(1, devices, drain_g, 0)
    for store in stores:
        store.wait()


def local(
    reflection,
    incidence,
    source_shift,
    source_weight,
    grid_map,
    pupil_mask,
    pupil_phase,
    tile_order,
):
    devices = lax.axis_size("ord")
    local_rows = reflection.shape[1]
    order2 = reflection.shape[2]
    sources = incidence.shape[2]
    side = pupil_mask.shape[0]
    samples = 2 * side
    assert source_shift.shape[0] == 1 and sources == devices
    chunks = 8
    cols, rows = lift_tables(side)
    table = band_table(PIX, side)
    hbm = pl.BlockSpec(memory_space=pltpu.HBM)
    part_rows = samples // devices
    dma = pltpu.SemaphoreType.DMA
    tile_rows = PIX // devices
    pieces = 4
    return pl.pallas_call(
        functools.partial(optics_kernel, devices=devices, chunks=chunks),
        out_shape=jax.ShapeDtypeStruct((tile_rows, 2, PIX), jnp.float32),
        in_specs=[hbm] * 12,
        out_specs=hbm,
        scratch_shapes=[
            pltpu.SMEM((1, 2), jnp.int32),
            pltpu.SMEM((1, 1), jnp.float32),
            pltpu.VMEM((devices // 2, 1, local_rows), jnp.int32),
            pltpu.VMEM((side, side), jnp.int32),
            pltpu.VMEM((2, side, side), jnp.float32),
            pltpu.VMEM(cols.shape, jnp.bfloat16),
            pltpu.VMEM(rows.shape, jnp.bfloat16),
            pltpu.SMEM(tile_order.shape, jnp.int32),
            pltpu.VMEM((devices, tile_rows, 2 * samples), jnp.bfloat16),
            pltpu.VMEM(table.shape, jnp.bfloat16),
            pltpu.VMEM((tile_rows, 2, PIX), jnp.float32),
            pltpu.VMEM((2, local_rows, order2), jnp.bfloat16),
            pltpu.VMEM((2, sources, order2), jnp.bfloat16),
            pltpu.VMEM((local_rows, 2 * sources), jnp.float32),
            pltpu.VMEM((devices, 2, local_rows), jnp.bfloat16),
            pltpu.VMEM((devices, 2, local_rows), jnp.bfloat16),
            pltpu.VMEM((2, side, samples), jnp.float32),
            pltpu.VMEM((devices, part_rows, 2 * samples), jnp.float32),
            pltpu.VMEM((2, devices, part_rows, 2 * samples), jnp.float32),
            dma((2, chunks)),
            dma((10,)),
            dma((1,)),
            dma((devices,)),
            dma((devices,)),
            dma((devices,)),
            dma((devices,)),
            dma((devices,)),
            dma((devices,)),
            dma((pieces,)),
        ],
        compiler_params=pltpu.CompilerParams(
            collective_id=0, has_side_effects=True, vmem_limit_bytes=67043328
        ),
    )(
        source_shift,
        source_weight.reshape(1, 1),
        reflection,
        jnp.transpose(incidence, (0, 2, 1)),
        grid_map.reshape(devices // 2, 1, local_rows),
        pupil_mask,
        pupil_phase,
        jnp.asarray(cols),
        jnp.asarray(rows),
        tile_order,
        jnp.asarray(table.reshape(devices, tile_rows, 2 * samples)),
        jnp.asarray(table),
    )


def solution(mesh):
    in_specs = (P(None, ("clip", "ord"), None), P(), P("ord", None), P("ord"), P(), P(), P(), P())
    out_specs = P(("clip", "ord"), None, None)
    return jax.shard_map(local, mesh=mesh, in_specs=in_specs, out_specs=out_specs, check_vma=False)
```

```python
import functools
import math

import jax
import jax.numpy as jnp
import numpy as np
from jax import lax
from jax.experimental import pallas as pl
from jax.experimental.pallas import tpu as pltpu
from jax.sharding import PartitionSpec as P

PIX = 1024
HIGHEST = lax.Precision.HIGHEST
NN = (((1,), (0,)), ((), ()))
NT = (((1,), (1,)), ((), ()))
MESH = pl.DeviceIdType.MESH


def turn_table(left, right, period):
    angles = np.mod(np.outer(left, right), period) * (2.0 * math.pi / period)
    return np.cos(angles), np.sin(angles)


def split_const(values):
    values = np.asarray(values, np.float32)
    high = values.astype(jnp.bfloat16)
    low = (values - high.astype(np.float32)).astype(jnp.bfloat16)
    return np.stack([high, low])


def lift_tables(grid_side):
    samples = 2 * grid_side
    frequency = np.arange(grid_side) - grid_side // 2
    cosine, sine = turn_table(frequency, np.arange(samples), samples)
    cols = np.block([[cosine, sine], [-sine, cosine]])
    rows = np.block([[cosine.T, -sine.T], [sine.T, cosine.T]])
    return split_const(cols), split_const(rows)


def band_table(pixels, grid_side):
    samples = 2 * grid_side
    difference = np.arange(1 - grid_side, grid_side)
    fine_cos, fine_sin = turn_table(np.arange(pixels), difference, pixels)
    coarse_cos, coarse_sin = turn_table(np.arange(samples), difference, samples)
    return np.concatenate(split_const((fine_cos @ coarse_cos.T + fine_sin @ coarse_sin.T) / samples), 1)


def split(values):
    high = values.astype(jnp.bfloat16)
    low = (values - high.astype(jnp.float32)).astype(jnp.bfloat16)
    return high, low


def dot3(left, right, dims):
    dot = functools.partial(lax.dot_general, dimension_numbers=dims, preferred_element_type=jnp.float32)
    return dot(left[0], right[0]) + (dot(left[0], right[1]) + dot(left[1], right[0]))


def optics_kernel(
    shift_hbm,
    weight_hbm,
    reflection_ref,
    incidence_ref,
    cells_hbm,
    mask_hbm,
    phase_hbm,
    cols_hbm,
    rows_hbm,
    tile_hbm,
    band_rows_hbm,
    band_cols_hbm,
    out_hbm,
    shift_ref,
    weight_ref,
    cells_ref,
    mask_ref,
    phase_ref,
    cols_ref,
    rows_ref,
    tile_ref,
    band_rows_ref,
    band_cols_ref,
    image_ref,
    refl_buf,
    inc_buf,
    acc_ref,
    send_buf,
    recv_buf,
    hit_ref,
    part_buf,
    gather_buf,
    load_sem,
    small_sem,
    own_sem,
    a_send,
    a_recv,
    r_send,
    r_recv,
    g_send,
    g_recv,
    out_sem,
    *,
    devices,
    chunks,
):
    me = lax.axis_index("ord")
    sources = inc_buf.shape[1]
    side = mask_ref.shape[0]
    samples = 2 * side
    depth = refl_buf.shape[2] // chunks

    def loads(c):
        span = pl.ds(c * depth, depth)
        return (
            pltpu.make_async_copy(incidence_ref.at[:, :, span], inc_buf.at[:, :, span], load_sem.at[0, c]),
            pltpu.make_async_copy(reflection_ref.at[:, :, span], refl_buf.at[:, :, span], load_sem.at[1, c]),
        )

    smalls = [
        pltpu.make_async_copy(source, target, small_sem.at[i])
        for i, (source, target) in enumerate(
            (
                (shift_hbm, shift_ref),
                (mask_hbm, mask_ref),
                (phase_hbm, phase_ref),
                (weight_hbm, weight_ref),
                (cells_hbm, cells_ref),
                (cols_hbm, cols_ref),
                (rows_hbm, rows_ref),
                (tile_hbm, tile_ref),
                (band_rows_hbm, band_rows_ref),
                (band_cols_hbm, band_cols_ref),
            )
        )
    ]
    for c in range(chunks):
        for load in loads(c):
            load.start()
    for small in smalls:
        small.start()

    barrier = pltpu.get_barrier_semaphore()

    def greet(j, carry):
        pl.semaphore_signal(barrier, inc=1, device_id={"ord": lax.rem(me + j, devices)}, device_id_type=MESH)
        return carry

    lax.fori_loop(1, devices, greet, 0)

    for c in range(chunks):
        inc_load, refl_load = loads(c)
        span = pl.ds(c * depth, depth)
        inc_load.wait()
        first = inc_buf[0, :, span]
        second = inc_buf[1, :, span]
        join_a = jnp.concatenate([first, second], 0)
        join_b = jnp.concatenate([-second, first], 0)
        refl_load.wait()
        step = lax.dot_general(join_a, refl_buf[0, :, span], NT, preferred_element_type=jnp.float32)
        step = step + lax.dot_general(join_b, refl_buf[1, :, span], NT, preferred_element_type=jnp.float32)
        if c == 0:
            acc_ref[...] = step
        else:
            acc_ref[...] += step

    lanes = 2 * sources
    to_row = lax.broadcasted_iota(jnp.int32, (lanes, lanes), 0)
    from_col = lax.broadcasted_iota(jnp.int32, (lanes, lanes), 1)
    turned = jnp.where(from_col == to_row // 2 + (to_row % 2) * sources, 1.0, 0.0).astype(jnp.bfloat16)
    by_source = lax.dot_general(
        turned, acc_ref[...].astype(jnp.bfloat16), NN, preferred_element_type=jnp.float32
    )
    for s in range(sources):
        send_buf[s] = by_source[2 * s : 2 * s + 2].astype(jnp.bfloat16)

    pl.semaphore_wait(barrier, devices - 1)

    def fan(source_of, target, send_sem, recv_sem):
        def copy_to(peer, sender):
            return pltpu.make_async_remote_copy(
                src_ref=source_of(peer),
                dst_ref=target.at[sender],
                send_sem=send_sem.at[peer],
                recv_sem=recv_sem.at[sender],
                device_id={"ord": peer},
                device_id_type=MESH,
            )

        def start(j, carry):
            copy_to(lax.rem(me + j, devices), me).start()
            return carry

        def wait_recv(sender):
            copy_to(sender, sender).wait_recv()

        def drain(j, carry):
            copy_to(lax.rem(me + j, devices), me).wait_send()
            return carry

        return start, wait_recv, drain

    start, wait_recv, drain_a = fan(lambda d: send_buf.at[d], recv_buf, a_send, a_recv)
    own = pltpu.make_async_copy(send_buf.at[me], recv_buf.at[me], own_sem.at[0])
    own.start()
    lax.fori_loop(1, devices, start, 0)

    for small in smalls:
        small.wait()
    shift_y = shift_ref[0, 0]
    shift_x = shift_ref[0, 1]
    opened = mask_ref[...].astype(jnp.float32) * (1.0 / side)
    planes = []
    for f in range(2):
        planes += [jnp.cos(phase_ref[f]) * opened, jnp.sin(phase_ref[f]) * opened]
    row_at = lax.broadcasted_iota(jnp.int32, (side, side), 0)
    col_at = lax.broadcasted_iota(jnp.int32, (side, side), 1)
    pick_row = jnp.where(col_at == row_at + shift_y, 1.0, 0.0)
    from_at = lax.broadcasted_iota(jnp.int32, (side, 2 * side), 0)
    to_at = lax.broadcasted_iota(jnp.int32, (side, 2 * side), 1)
    half = jnp.where(to_at >= side, 1, 0)
    hit = from_at == to_at - half * side + shift_x
    pick_cos = jnp.where(hit, 1.0, 0.0)
    pick_sin = jnp.where(hit, jnp.where(half == 1, 1.0, -1.0), 0.0)
    windows = []
    for f in range(2):
        for kind, pick in ((0, pick_cos), (1, pick_sin)):
            moved = lax.dot_general(pick_row, planes[2 * f + kind], NN, precision=HIGHEST, preferred_element_type=jnp.float32)
            windows.append(lax.dot_general(moved, pick, NN, precision=HIGHEST, preferred_element_type=jnp.float32))


    local_rows = recv_buf.shape[2]
    per_pol = devices // 2
    cell_at = lax.broadcasted_iota(jnp.int32, (side, local_rows), 0)
    for q in range(per_pol):
        cells = cells_ref[q]
        cell_y = cells // side
        hit_ref[q, 0] = jnp.where(cell_at == cell_y, 1.0, 0.0).astype(jnp.bfloat16)
        hit_ref[q, 1] = jnp.where(cell_at == cells - cell_y * side, 1.0, 0.0).astype(jnp.bfloat16)

    def take(j, carry):
        wait_recv(lax.rem(me + j, devices))
        return carry

    lax.fori_loop(1, devices, take, 0)
    own.wait()
    grid = None
    for q in range(per_pol):
        hit_x = hit_ref[q, 1]
        spread = []
        for p in range(2):
            values = recv_buf[p * per_pol + q]
            spread += [hit_x * values[0:1], hit_x * values[1:2]]
        term = lax.dot_general(
            hit_ref[q, 0], jnp.concatenate(spread, 0), NT, preferred_element_type=jnp.float32
        )
        grid = term if grid is None else grid + term

    amps = []
    for f in range(2):
        for p in range(2):
            cells = grid[:, p * samples : (p + 1) * samples]
            swapped = jnp.concatenate([cells[:, side:], cells[:, :side]], 1)
            amps.append(cells * windows[2 * f] + swapped * windows[2 * f + 1])
    stacked = split(jnp.concatenate(amps, 0))
    halves = dot3(stacked, (cols_ref[0], cols_ref[1]), NN)
    columns = jnp.concatenate(
        [
            jnp.concatenate(
                [
                    halves[i * side : (i + 1) * side, :samples],
                    halves[i * side : (i + 1) * side, samples:],
                ],
                0,
            )
            for i in range(4)
        ],
        1,
    )
    fields = dot3((rows_ref[0], rows_ref[1]), split(columns), NN)
    powers = fields[:samples] * fields[:samples] + fields[samples:] * fields[samples:]
    weight = weight_ref[0, 0] * (1.0 / sources)
    summed = (
        jnp.concatenate(
            [
                powers[:, :samples] + powers[:, samples : 2 * samples],
                powers[:, 2 * samples : 3 * samples] + powers[:, 3 * samples :],
            ],
            1,
        )
        * weight
    )
    part_rows = part_buf.shape[1]
    part_buf[...] = summed.reshape(devices, part_rows, 2 * samples)

    start, wait_recv_r, drain_r = fan(lambda d: part_buf.at[d], gather_buf.at[0], r_send, r_recv)
    lax.fori_loop(1, devices, start, 0)

    def add(j, total):
        r = lax.rem(me + j, devices)
        wait_recv_r(r)
        return total + gather_buf[0, r]

    total = lax.fori_loop(1, devices, add, part_buf[me])
    gather_buf[1, me] = total

    start, wait_recv_g, drain_g = fan(lambda d: gather_buf.at[1, me], gather_buf.at[1], g_send, g_recv)
    lax.fori_loop(1, devices, start, 0)

    def arrive(j, carry):
        wait_recv_g(lax.rem(me + j, devices))
        return carry

    lax.fori_loop(1, devices, arrive, 0)
    tile_rows, _, pixels = image_ref.shape
    pieces = out_sem.shape[0]
    lift = band_rows_ref[tile_ref[me]]
    high, low = split(gather_buf[1].reshape(samples, 2 * samples))
    partial = jnp.dot(lift, jnp.concatenate([high, high], 0), preferred_element_type=jnp.float32)
    partial = partial + jnp.dot(lift[:, :samples], low, preferred_element_type=jnp.float32)
    high, low = split(jnp.concatenate([partial[:, :samples], partial[:, samples:]], 0))
    twice = jnp.concatenate([high, high], 1)
    width = pixels // pieces
    stores = []
    for i in range(pieces):
        span = pl.ds(i * width, width)
        table = band_cols_ref[span, :]
        piece = lax.dot_general(twice, table, NT, preferred_element_type=jnp.float32)
        piece = piece + lax.dot_general(low, table[:, :samples], NT, preferred_element_type=jnp.float32)
        image_ref[:, 0, span] = piece[:tile_rows]
        image_ref[:, 1, span] = piece[tile_rows:]
        store = pltpu.make_async_copy(image_ref.at[:, :, span], out_hbm.at[:, :, span], out_sem.at[i])
        store.start()
        stores.append(store)
    lax.fori_loop(1, devices, drain_a, 0)
    lax.fori_loop(1, devices, drain_r, 0)
    lax.fori_loop(1, devices, drain_g, 0)
    for store in stores:
        store.wait()


def local(
    reflection,
    incidence,
    source_shift,
    source_weight,
    grid_map,
    pupil_mask,
    pupil_phase,
    tile_order,
):
    devices = lax.axis_size("ord")
    local_rows = reflection.shape[1]
    order2 = reflection.shape[2]
    sources = incidence.shape[2]
    side = pupil_mask.shape[0]
    samples = 2 * side
    assert source_shift.shape[0] == 1 and sources == devices
    chunks = 16
    cols, rows = lift_tables(side)
    table = band_table(PIX, side)
    hbm = pl.BlockSpec(memory_space=pltpu.HBM)
    part_rows = samples // devices
    dma = pltpu.SemaphoreType.DMA
    tile_rows = PIX // devices
    pieces = 4
    return pl.pallas_call(
        functools.partial(optics_kernel, devices=devices, chunks=chunks),
        out_shape=jax.ShapeDtypeStruct((tile_rows, 2, PIX), jnp.float32),
        in_specs=[hbm] * 12,
        out_specs=hbm,
        scratch_shapes=[
            pltpu.SMEM((1, 2), jnp.int32),
            pltpu.SMEM((1, 1), jnp.float32),
            pltpu.VMEM((devices // 2, 1, local_rows), jnp.int32),
            pltpu.VMEM((side, side), jnp.int32),
            pltpu.VMEM((2, side, side), jnp.float32),
            pltpu.VMEM(cols.shape, jnp.bfloat16),
            pltpu.VMEM(rows.shape, jnp.bfloat16),
            pltpu.SMEM(tile_order.shape, jnp.int32),
            pltpu.VMEM((devices, tile_rows, 2 * samples), jnp.bfloat16),
            pltpu.VMEM(table.shape, jnp.bfloat16),
            pltpu.VMEM((tile_rows, 2, PIX), jnp.float32),
            pltpu.VMEM((2, local_rows, order2), jnp.bfloat16),
            pltpu.VMEM((2, sources, order2), jnp.bfloat16),
            pltpu.VMEM((2 * sources, local_rows), jnp.float32),
            pltpu.VMEM((devices, 2, local_rows), jnp.bfloat16),
            pltpu.VMEM((devices, 2, local_rows), jnp.bfloat16),
            pltpu.VMEM((devices // 2, 2, side, local_rows), jnp.bfloat16),
            pltpu.VMEM((devices, part_rows, 2 * samples), jnp.float32),
            pltpu.VMEM((2, devices, part_rows, 2 * samples), jnp.float32),
            dma((2, chunks)),
            dma((10,)),
            dma((1,)),
            dma((devices,)),
            dma((devices,)),
            dma((devices,)),
            dma((devices,)),
            dma((devices,)),
            dma((devices,)),
            dma((pieces,)),
        ],
        compiler_params=pltpu.CompilerParams(
            collective_id=0, has_side_effects=True, vmem_limit_bytes=67043328
        ),
    )(
        source_shift,
        source_weight.reshape(1, 1),
        reflection,
        jnp.transpose(incidence, (0, 2, 1)),
        grid_map.reshape(devices // 2, 1, local_rows),
        pupil_mask,
        pupil_phase,
        jnp.asarray(cols),
        jnp.asarray(rows),
        tile_order,
        jnp.asarray(table.reshape(devices, tile_rows, 2 * samples)),
        jnp.asarray(table),
    )


def solution(mesh):
    in_specs = (P(None, ("clip", "ord"), None), P(), P("ord", None), P("ord"), P(), P(), P(), P())
    out_specs = P(("clip", "ord"), None, None)
    return jax.shard_map(local, mesh=mesh, in_specs=in_specs, out_specs=out_specs, check_vma=False)
```
